32 devices in a mesh: trow: 4 (over y, core), tcol: 8 (over z, x).
Axes of the slice: x: 2, y: 2, z: 4, core: 2. Of those that a mesh axis runs over, the one named last changes fastest.
Arguments:
- response: bfloat16 [4096, 16384], P('trow', 'tcol'), may hold values from -0.046875 to 0.046875
- test_matrix: bfloat16 [1024, 192], P(('trow', 'tcol')), may hold values from -6 to 6
- slopes: bfloat16 [16384, 256], P('tcol', 'trow'), may hold values from -6 to 6
- ranks: int32 [4, 16], P('trow', 'tcol'), may hold values from 16 to 192, as said below
Outputs:
- commands: float32 [4096, 256], P(('trow', 'tcol'))
The draws below stay inside these ranges and needn't reach their ends.
Inputs may be any that keep to these rules, and one draw needn't show every extreme that they name: ranks of tiles near the diagonal tend to be higher, and every tile's sketch has full column rank and is well conditioned.
All inputs are finite; a program needn't handle non-finite values.
Results may differ from the reference program's by a relative error of at most 0.014.
Values may be sent and summed in bfloat16 or wider, within the bound.
A program may use at most 64 MiB of HBM per device.

```python
import jax
import jax.numpy as jnp
from jax import lax

TILE = 1024
SKETCH = 192
FRAMES = 256
TROWS = 4
TCOLS = 16
COMMANDS = 4096
SLOPES = 16384


def draw_ranks(key, part):
    lowest = SKETCH // 12
    rowidx = jnp.arange(TROWS, dtype=jnp.int32)[:, None]
    colidx = jnp.arange(TCOLS, dtype=jnp.int32)[None, :]
    distance = jnp.abs(colidx * TROWS - rowidx * TCOLS)
    whole = TROWS * TCOLS
    highest = lowest + (SKETCH - lowest) * whole // (whole + 4 * distance)
    raw = jax.random.randint(jax.random.fold_in(key, 17), (TROWS, TCOLS), 0, 1048576, dtype=jnp.int32)
    values = lowest + raw % (highest - lowest + 1)
    values = values.at[0, 0].set(SKETCH)
    values = values.at[TROWS - 1, 0].set(lowest)
    return values.astype(jnp.int32)


def block_scale(rng, extent, cuts, least, high):
    loudness, own = 1.0, jax.random.fold_in(rng, 6)
    for dim, parts in cuts:
        heights = jnp.exp(jax.random.uniform(jax.random.fold_in(own, dim), (parts,), jnp.float32, least / len(cuts), high / len(cuts)))
        loudness = loudness * jnp.repeat(heights, extent[dim] // parts).reshape([-1 if axis == dim else 1 for axis in range(len(extent))])
    return loudness


def centred(rng, extent, scale, bound, pieces=(), kind=jnp.bfloat16):
    level = block_scale(rng, extent, pieces, -0.22, 0.18) if pieces else 1.0
    drawn = jax.random.normal(rng, extent, jnp.float32) * scale * level
    return jnp.minimum(jnp.maximum(drawn, -bound), bound).astype(kind)


def setup_inputs(seed: int = 0) -> dict:
    key_of = jax.random.split(jax.random.key(seed), 5)
    response = centred(key_of[0], (COMMANDS, SLOPES), SLOPES ** -0.5, 0.046875, ((0, 4), (1, 8)))
    test_matrix = centred(key_of[1], (TILE, SKETCH), 1.0, 6.0, ((0, 32),))
    slopes = centred(key_of[2], (SLOPES, FRAMES), 1.0, 6.0, ((0, 8), (1, 4)))
    ranks = draw_ranks(jax.random.fold_in(key_of[4], 71), 0)
    return dict(response=response, test_matrix=test_matrix, slopes=slopes, ranks=ranks)


def reference(response, test_matrix, slopes, ranks):
    highest = lax.Precision.HIGHEST
    omega = test_matrix.astype(jnp.float32)
    frame_tiles = slopes.astype(jnp.float32).reshape(TCOLS, TILE, FRAMES)
    slots = jnp.arange(SKETCH, dtype=jnp.int32)

    def one_row(index):
        band = lax.dynamic_slice_in_dim(response, (index * TILE).astype(jnp.int32), TILE, 0)
        tiles = band.astype(jnp.float32).reshape(TILE, TCOLS, TILE).transpose(1, 0, 2)
        sketch = jnp.einsum('cij,jk->cik', tiles, omega, precision=highest)
        gram = jnp.einsum('cik,cil->ckl', sketch, sketch, precision=highest)
        chol = jnp.linalg.cholesky(gram)
        basis = jax.scipy.linalg.solve_triangular(chol, jnp.swapaxes(sketch, 1, 2), lower=True)
        row_ranks = lax.dynamic_index_in_dim(ranks, index, 0, keepdims=False)
        keep = (slots[None, :] < row_ranks[:, None]).astype(jnp.float32)
        basis = (basis * keep[:, :, None]).astype(jnp.bfloat16)
        factor = jnp.einsum('csi,cij->csj', basis.astype(jnp.float32), tiles, precision=highest).astype(jnp.bfloat16)
        coeff = jnp.einsum('csj,cjf->csf', factor.astype(jnp.float32), frame_tiles, precision=highest).astype(jnp.bfloat16)
        return jnp.einsum('csi,csf->if', basis.astype(jnp.float32), coeff.astype(jnp.float32), precision=highest)
    blocks = lax.map(one_row, jnp.arange(TROWS, dtype=jnp.int32))
    return blocks.reshape(TROWS * TILE, FRAMES)
```

```python
import functools

import jax
import jax.numpy as jnp
from jax import lax
from jax.experimental import pallas as pl
from jax.experimental.pallas import tpu as pltpu
from jax.sharding import PartitionSpec as P

MESH = pl.DeviceIdType.MESH
F32 = jnp.float32
BF16 = jnp.bfloat16
HIGHEST = lax.Precision.HIGHEST
BLOCK = 64


def dot(a, b, ca, cb, precision=None):
    return lax.dot_general(
        a, b, (((ca,), (cb,)), ((), ())), precision=precision, preferred_element_type=F32
    )


def split_halves(x, low):
    zero = jnp.zeros_like(x)
    return jnp.concatenate([jnp.where(low, x, zero), jnp.where(low, zero, x)], axis=0)


def invert_block(x):
    lane = lax.broadcasted_iota(jnp.int32, x.shape, 1)
    for k in range(BLOCK):
        where = jnp.where(lane < BLOCK, k, BLOCK + k)
        column = jnp.take_along_axis(x, where, axis=1)
        row = x[k : k + 1, :]
        pivot = column[k : k + 1, :]
        x = x - column * (row * (1.0 / (1.0 + pivot)))
    return x


def kernel(
    nr, nc, resp, tm, sl, ranks, out,
    a_v, om, own, fr, s_b, w_v, b_v, part, land,
    a_sem, o_sem, f_sem, s1, r1, s2, r2, s3, r3, s4, r4,
):
    r, c = lax.axis_index("trow"), lax.axis_index("tcol")
    width = a_v.shape[0]
    sketch = tm.shape[1]
    blocks = sketch // BLOCK
    tile_cols = a_v.shape[1] // width
    local = sl.shape[1]
    load_a = pltpu.make_async_copy(resp, a_v, a_sem)
    load_a.start()
    own_om = pltpu.make_async_copy(tm, om.at[r, c], o_sem)
    own_om.start()
    for t in range(tile_cols):
        own[:, t * local : (t + 1) * local] = sl[t * width : (t + 1) * width, :]
    barrier = pltpu.get_barrier_semaphore()
    for d in range(1, nc):
        pl.semaphore_signal(barrier, inc=1, device_id=(r, lax.rem(c + d, nc)), device_id_type=MESH)
    for e in range(1, nr):
        pl.semaphore_signal(barrier, inc=1, device_id=(lax.rem(r + e, nr), c), device_id_type=MESH)
    pl.semaphore_wait(barrier, nc - 1 + nr - 1)
    first = []
    for d in range(1, nc):
        cp = pltpu.make_async_remote_copy(
            tm, om.at[r, c], s1.at[d - 1], r1.at[d - 1],
            device_id=(r, lax.rem(c + d, nc)), device_id_type=MESH,
        )
        cp.start()
        first.append(cp)
    own_om.wait()
    for cp in first:
        cp.wait_recv()
    second, third = [], []
    for e in range(1, nr):
        cp = pltpu.make_async_remote_copy(
            om.at[r], om.at[r], s2.at[e - 1], r2.at[e - 1],
            device_id=(lax.rem(r + e, nr), c), device_id_type=MESH,
        )
        cp.start()
        second.append(cp)
    own_fr = pltpu.make_async_copy(own, fr.at[r], f_sem)
    own_fr.start()
    for e in range(1, nr):
        cp = pltpu.make_async_remote_copy(
            own, fr.at[r], s3.at[e - 1], r3.at[e - 1],
            device_id=(lax.rem(r + e, nr), c), device_id_type=MESH,
        )
        cp.start()
        third.append(cp)
    load_a.wait()
    for cp in second:
        cp.wait_recv()
    omega = om[...].astype(F32).reshape(width, sketch).astype(BF16)

    slot = lax.broadcasted_iota(jnp.int32, (1, sketch), 1)
    grams = []
    for t in range(tile_cols):
        s = dot(a_v[:, t * width : (t + 1) * width], omega, 1, 0)
        norm = jnp.sum(s * s, axis=0, keepdims=True)
        scale = jnp.where(slot < ranks[0, t], lax.rsqrt(norm), 0.0)
        hat = (s * scale).astype(BF16)
        s_b[t] = hat
        grams.append(dot(hat, hat, 0, 0))

    half = lax.broadcasted_iota(jnp.int32, (sketch, 2 * BLOCK), 1)
    rows = lax.broadcasted_iota(jnp.int32, (sketch, 2 * BLOCK), 0)
    low = half < BLOCK
    for j in range(blocks):
        x = jnp.concatenate([g[:, j * BLOCK : (j + 1) * BLOCK] for g in grams], axis=1)
        index = jnp.where(low, half, half - BLOCK) + j * BLOCK
        limit = jnp.where(low, ranks[0, 0], ranks[0, 1])
        b_v[j] = jnp.where((rows == index) & (index < limit), x - 1.0, x)

    low_b = lax.broadcasted_iota(jnp.int32, (BLOCK, 2 * BLOCK), 1) < BLOCK
    for k in range(blocks):
        span = slice(k * BLOCK, (k + 1) * BLOCK)
        square = invert_block(b_v[k, span, :])
        whole_k = b_v[k]
        mid = whole_k - dot(whole_k, split_halves(square, low_b), 1, 0, HIGHEST)
        rights = [split_halves(b_v[j, span, :], low_b) for j in range(blocks)]
        for j in range(blocks):
            b_v[j] = b_v[j] - dot(mid, rights[j], 1, 0, HIGHEST)

    own_fr.wait()
    for cp in third:
        cp.wait_recv()
    frames = nr * local
    for t in range(tile_cols):
        s_t = jnp.concatenate(
            [fr[q, :, t * local : (t + 1) * local] for q in range(nr)], axis=1
        )
        y = dot(a_v[:, t * width : (t + 1) * width], s_t, 1, 0).astype(BF16)
        w_v[t] = dot(s_b[t], y, 0, 0)

    full = jnp.concatenate([b_v[j] for j in range(blocks)], axis=1)
    stack = []
    for j in range(blocks):
        span = slice(j * BLOCK, (j + 1) * BLOCK)
        w0, w1 = w_v[0, span, :], w_v[1, span, :]
        zero = jnp.zeros_like(w0)
        stack.append(jnp.concatenate([w0, zero], axis=1))
        stack.append(jnp.concatenate([zero, w1], axis=1))
    corr = dot(full, jnp.concatenate(stack, axis=0), 1, 0, HIGHEST)
    ds = [
        (w_v[t] - corr[:, t * frames : (t + 1) * frames]).astype(BF16) for t in range(tile_cols)
    ]

    share = width // nc
    sends = []

    def chunk(at):
        rows_at = pl.ds(pl.multiple_of(at * share, share), share)
        return sum(dot(s_b[t, rows_at, :], ds[t], 1, 0) for t in range(tile_cols))

    for d in range(1, nc):
        to = lax.rem(c + d, nc)
        part[d - 1] = chunk(to).astype(BF16)
        cp = pltpu.make_async_remote_copy(
            part.at[d - 1], land.at[d - 1], s4.at[d - 1], r4.at[d - 1],
            device_id=(r, to), device_id_type=MESH,
        )
        sends.append(cp)
        if d > 1:
            sends[d - 2].start()
    total = chunk(c)
    sends[-1].start()
    for cp, n in zip(sends, range(nc)):
        cp.wait_recv()
        total = total + land[n].astype(F32)
    out[...] = total
    for cp in first + second + third + sends:
        cp.wait_send()


def on_device(nr, nc, response, test_matrix, slopes, ranks):
    rows, cols = response.shape
    tile_rows, tile_cols = ranks.shape
    width = rows // tile_rows
    m, sketch = test_matrix.shape
    local = slopes.shape[1]
    frames = local * nr
    share = width // nc
    dma = pltpu.SemaphoreType.DMA
    return pl.pallas_call(
        functools.partial(kernel, nr, nc),
        out_shape=jax.ShapeDtypeStruct((share, frames), F32),
        in_specs=[
            pl.BlockSpec(memory_space=pl.ANY),
            pl.BlockSpec(memory_space=pltpu.VMEM),
            pl.BlockSpec(memory_space=pltpu.VMEM),
            pl.BlockSpec(memory_space=pltpu.SMEM),
        ],
        out_specs=pl.BlockSpec(memory_space=pltpu.VMEM),
        scratch_shapes=[
            pltpu.VMEM((rows, cols), BF16),
            pltpu.VMEM((nr, nc, m, sketch), BF16),
            pltpu.VMEM((width, tile_cols * local), BF16),
            pltpu.VMEM((nr, width, tile_cols * local), BF16),
            pltpu.VMEM((tile_cols, width, sketch), BF16),
            pltpu.VMEM((tile_cols, sketch, frames), F32),
            pltpu.VMEM((sketch // BLOCK, sketch, 2 * BLOCK), F32),
            pltpu.VMEM((nc - 1, share, frames), BF16),
            pltpu.VMEM((nc - 1, share, frames), BF16),
            dma, dma, dma,
            dma((nc - 1,)), dma((nc - 1,)),
            dma((nr - 1,)), dma((nr - 1,)),
            dma((nr - 1,)), dma((nr - 1,)),
            dma((nc - 1,)), dma((nc - 1,)),
        ],
        compiler_params=pltpu.CompilerParams(
            collective_id=0, has_side_effects=True, vmem_limit_bytes=60 * 1024 * 1024
        ),
    )(response, test_matrix, slopes, ranks)


def solution(mesh):
    nr, nc = mesh.shape["trow"], mesh.shape["tcol"]
    return jax.shard_map(
        functools.partial(on_device, nr, nc),
        mesh=mesh,
        in_specs=(
            P("trow", "tcol"),
            P(("trow", "tcol"), None),
            P("tcol", "trow"),
            P("trow", "tcol"),
        ),
        out_specs=P(("trow", "tcol"), None),
        check_vma=False,
    )
```

```python
import functools

import jax
import jax.numpy as jnp
from jax import lax
from jax.experimental import pallas as pl
from jax.experimental.pallas import tpu as pltpu
from jax.sharding import PartitionSpec as P

MESH = pl.DeviceIdType.MESH
F32 = jnp.float32
BF16 = jnp.bfloat16
HIGHEST = lax.Precision.HIGHEST
BLOCK = 64
PANEL = 8


def dot(a, b, ca, cb, precision=None):
    return lax.dot_general(
        a, b, (((ca,), (cb,)), ((), ())), precision=precision, preferred_element_type=F32
    )


def split_halves(x, low):
    zero = jnp.zeros_like(x)
    return jnp.concatenate([jnp.where(low, x, zero), jnp.where(low, zero, x)], axis=0)


def invert_block(x):
    base = jnp.where(lax.broadcasted_iota(jnp.int32, (PANEL, x.shape[1]), 1) < BLOCK, 0, BLOCK)
    for at in range(0, BLOCK, PANEL):
        picks = [base + (at + i) for i in range(PANEL)]
        rows = x[at : at + PANEL, :]
        cols = [jnp.take_along_axis(rows, pick, axis=1) for pick in picks]
        for i in range(0, PANEL, 2):
            c0, c1 = cols[i], cols[i + 1]
            p00 = 1.0 + c0[i : i + 1, :]
            p01 = c1[i : i + 1, :]
            p11 = 1.0 + c1[i + 1 : i + 2, :]
            inv = 1.0 / (p00 * p11 - p01 * p01)
            m00, m01, m11 = p11 * inv, -p01 * inv, p00 * inv

            def clear(v):
                v0, v1 = v[i : i + 1, :], v[i + 1 : i + 2, :]
                return v - (c0 * (m00 * v0 + m01 * v1) + c1 * (m01 * v0 + m11 * v1))

            rows = clear(rows)
            for j in range(i + 2, PANEL):
                cols[j] = clear(cols[j])
        pieces = []
        for top in range(0, BLOCK, PANEL):
            piece = x[top : top + PANEL, :]
            delta = None
            for i in range(PANEL):
                term = jnp.take_along_axis(piece, picks[i], axis=1) * rows[i : i + 1, :]
                delta = term if delta is None else delta + term
            pieces.append(piece - delta)
        x = jnp.concatenate(pieces, axis=0)
    return x


def kernel(
    nr, nc, resp, tm, sl, ranks, out,
    a_v, om, fr, s_v, s_b, s_t, w_v, b_v, keep, part1, land1, part2, land2,
    a_sem, o_sem, f_sem, s1, r1, s2, r2, s3, r3, s4, r4, s5, r5,
):
    r, c = lax.axis_index("trow"), lax.axis_index("tcol")
    width = a_v.shape[0]
    sketch = tm.shape[1]
    blocks = sketch // BLOCK
    tile_cols = a_v.shape[1] // width
    local = sl.shape[0]
    deep = width // nr
    load_a = pltpu.make_async_copy(resp, a_v, a_sem)
    load_a.start()
    own_om = pltpu.make_async_copy(tm, om.at[r, c], o_sem)
    own_om.start()
    own_fr = pltpu.make_async_copy(sl, fr.at[r], f_sem)
    own_fr.start()
    barrier = pltpu.get_barrier_semaphore()
    for d in range(1, nc):
        pl.semaphore_signal(barrier, inc=1, device_id=(r, lax.rem(c + d, nc)), device_id_type=MESH)
    for e in range(1, nr):
        pl.semaphore_signal(barrier, inc=1, device_id=(lax.rem(r + e, nr), c), device_id_type=MESH)
    pl.semaphore_wait(barrier, nc - 1 + nr - 1)
    first = []
    for d in range(1, nc):
        cp = pltpu.make_async_remote_copy(
            tm, om.at[r, c], s1.at[d - 1], r1.at[d - 1],
            device_id=(r, lax.rem(c + d, nc)), device_id_type=MESH,
        )
        cp.start()
        first.append(cp)
    own_om.wait()
    for cp in first:
        cp.wait_recv()

    mate = r + 1 - 2 * lax.rem(r, 2)
    far = nr // 2

    def shift(e):
        return lax.rem(r + 2 * e, nr)

    def unshift(e):
        return lax.rem(r - 2 * e + nr, nr)

    def push(src, dst, send, recv, n, to):
        cp = pltpu.make_async_remote_copy(
            src, dst, send.at[n], recv.at[n], device_id=(to, c), device_id_type=MESH
        )
        cp.start()
        return cp

    second = [push(om.at[r], om.at[r], s2, r2, e, shift(e)) for e in range(1, far)]
    second.insert(0, push(om.at[r], om.at[r], s2, r2, 0, mate))
    third = [push(sl, fr.at[r], s3, r3, e, shift(e)) for e in range(1, far)]
    third.insert(0, push(sl, fr.at[r], s3, r3, 0, mate))
    load_a.wait()

    def add_block(q, fresh):
        omega = om[q].astype(F32).reshape(deep, sketch).astype(BF16)
        for t in range(tile_cols):
            at = pl.ds(pl.multiple_of(t * width + q * deep, 128), deep)
            term = dot(a_v[:, at], omega, 1, 0)
            s_v[t] = term if fresh else s_v[t] + term

    add_block(r, True)
    for e in range(1, far):
        second[e].wait_recv()
        q = unshift(e)
        second.append(push(om.at[q], om.at[q], s2, r2, far - 1 + e, mate))
    second[0].wait_recv()
    add_block(mate, False)
    for e in range(1, far):
        add_block(unshift(e), False)
    for e in range(1, far):
        second[far - 1 + e].wait_recv()
        q = unshift(e)
        add_block(q + 1 - 2 * lax.rem(q, 2), False)

    slot = lax.broadcasted_iota(jnp.int32, (1, sketch), 1)
    grams = []
    for t in range(tile_cols):
        s = s_v[t]
        norm = jnp.sum(s * s, axis=0, keepdims=True)
        scale = jnp.where(slot < ranks[0, t], lax.rsqrt(norm), 0.0)
        hat = (s * scale).astype(BF16)
        s_b[t] = hat
        turned = hat.T
        s_t[t] = turned
        grams.append(dot(turned, hat, 1, 0))

    half = lax.broadcasted_iota(jnp.int32, (sketch, 2 * BLOCK), 1)
    rows = lax.broadcasted_iota(jnp.int32, (sketch, 2 * BLOCK), 0)
    low = half < BLOCK
    for j in range(blocks):
        x = jnp.concatenate([g[:, j * BLOCK : (j + 1) * BLOCK] for g in grams], axis=1)
        index = jnp.where(low, half, half - BLOCK) + j * BLOCK
        limit = jnp.where(low, ranks[0, 0], ranks[0, 1])
        b_v[j] = jnp.where((rows == index) & (index < limit), x - 1.0, x)

    low_b = lax.broadcasted_iota(jnp.int32, (BLOCK, 2 * BLOCK), 1) < BLOCK
    for k in range(blocks):
        span = slice(k * BLOCK, (k + 1) * BLOCK)
        square = invert_block(b_v[k, span, :])
        whole_k = b_v[k]
        mid = whole_k - dot(whole_k, split_halves(square, low_b), 1, 0, HIGHEST)
        rights = [split_halves(b_v[j, span, :], low_b) for j in range(blocks)]
        for j in range(blocks):
            b_v[j] = b_v[j] - dot(mid, rights[j], 1, 0, HIGHEST)
        if k == 0:
            for e in range(1, far):
                third[e].wait_recv()
                q = unshift(e)
                third.append(push(fr.at[q], fr.at[q], s3, r3, far - 1 + e, mate))

    own_fr.wait()
    third[0].wait_recv()
    for e in range(1, far):
        third[far - 1 + e].wait_recv()
    frames = nr * local
    for t in range(tile_cols):
        s = fr[:, :, t * width : (t + 1) * width].reshape(frames, width)
        y = dot(a_v[:, t * width : (t + 1) * width], s, 1, 1).astype(BF16)
        w_v[t] = dot(s_t[t], y, 1, 0)

    full = jnp.concatenate([b_v[j] for j in range(blocks)], axis=1)
    stack = []
    for j in range(blocks):
        span = slice(j * BLOCK, (j + 1) * BLOCK)
        w0, w1 = w_v[0, span, :], w_v[1, span, :]
        zero = jnp.zeros_like(w0)
        stack.append(jnp.concatenate([w0, zero], axis=1))
        stack.append(jnp.concatenate([zero, w1], axis=1))
    corr = dot(full, jnp.concatenate(stack, axis=0), 1, 0, HIGHEST)
    ds = [
        (w_v[t] - corr[:, t * frames : (t + 1) * frames]).astype(BF16) for t in range(tile_cols)
    ]

    share = width // nc
    pairs = nc // 2
    side = lax.rem(c, 2)
    near = c + 1 - 2 * side
    order = list(range(1, pairs)) + [0]

    def group(e):
        return 2 * lax.rem(c // 2 + e, pairs)

    def chunk(at):
        rows_at = pl.ds(pl.multiple_of(at * share, share), share)
        return sum(dot(s_b[t, rows_at, :], ds[t], 1, 0) for t in range(tile_cols))

    across = []
    for n, e in enumerate(order):
        part1[n] = chunk(group(e) + 1 - side).astype(BF16)
        keep[n] = chunk(group(e) + side)
        cp = pltpu.make_async_remote_copy(
            part1.at[n], land1.at[n], s4.at[n], r4.at[n],
            device_id=(r, near), device_id_type=MESH,
        )
        cp.start()
        across.append(cp)
    along = []
    for n in range(pairs - 1):
        across[n].wait_recv()
        part2[n] = (keep[n] + land1[n].astype(F32)).astype(BF16)
        cp = pltpu.make_async_remote_copy(
            part2.at[n], land2.at[n], s5.at[n], r5.at[n],
            device_id=(r, group(order[n]) + side), device_id_type=MESH,
        )
        cp.start()
        along.append(cp)
    across[-1].wait_recv()
    total = keep[pairs - 1] + land1[pairs - 1].astype(F32)
    for n in range(pairs - 1):
        along[n].wait_recv()
        total = total + land2[n].astype(F32)
    out[...] = total
    for cp in first + second + third + across + along:
        cp.wait_send()


def on_device(nr, nc, response, test_matrix, slopes, ranks):
    rows, cols = response.shape
    tile_rows, tile_cols = ranks.shape
    width = rows // tile_rows
    m, sketch = test_matrix.shape
    slopes = slopes.T
    local = slopes.shape[0]
    frames = local * nr
    share = width // nc
    pairs = nc // 2
    dma = pltpu.SemaphoreType.DMA
    return pl.pallas_call(
        functools.partial(kernel, nr, nc),
        out_shape=jax.ShapeDtypeStruct((share, frames), F32),
        in_specs=[
            pl.BlockSpec(memory_space=pl.ANY),
            pl.BlockSpec(memory_space=pltpu.VMEM),
            pl.BlockSpec(memory_space=pltpu.VMEM),
            pl.BlockSpec(memory_space=pltpu.SMEM),
        ],
        out_specs=pl.BlockSpec(memory_space=pltpu.VMEM),
        scratch_shapes=[
            pltpu.VMEM((rows, cols), BF16),
            pltpu.VMEM((nr, nc, m, sketch), BF16),
            pltpu.VMEM((nr, local, cols), BF16),
            pltpu.VMEM((tile_cols, width, sketch), F32),
            pltpu.VMEM((tile_cols, width, sketch), BF16),
            pltpu.VMEM((tile_cols, sketch, width), BF16),
            pltpu.VMEM((tile_cols, sketch, frames), F32),
            pltpu.VMEM((sketch // BLOCK, sketch, 2 * BLOCK), F32),
            pltpu.VMEM((pairs, share, frames), F32),
            pltpu.VMEM((pairs, share, frames), BF16),
            pltpu.VMEM((pairs, share, frames), BF16),
            pltpu.VMEM((pairs - 1, share, frames), BF16),
            pltpu.VMEM((pairs - 1, share, frames), BF16),
            dma, dma, dma,
            dma((nc - 1,)), dma((nc - 1,)),
            dma((nr - 1,)), dma((nr - 1,)),
            dma((nr - 1,)), dma((nr - 1,)),
            dma((pairs,)), dma((pairs,)),
            dma((pairs - 1,)), dma((pairs - 1,)),
        ],
        compiler_params=pltpu.CompilerParams(
            collective_id=0, has_side_effects=True, vmem_limit_bytes=60 * 1024 * 1024
        ),
    )(response, test_matrix, slopes, ranks)


def solution(mesh):
    nr, nc = mesh.shape["trow"], mesh.shape["tcol"]
    return jax.shard_map(
        functools.partial(on_device, nr, nc),
        mesh=mesh,
        in_specs=(
            P("trow", "tcol"),
            P(("trow", "tcol"), None),
            P("tcol", "trow"),
            P("trow", "tcol"),
        ),
        out_specs=P(("trow", "tcol"), None),
        check_vma=False,
    )
```

```python
import functools

import jax
import jax.numpy as jnp
from jax import lax
from jax.experimental import pallas as pl
from jax.experimental.pallas import tpu as pltpu
from jax.sharding import PartitionSpec as P

MESH = pl.DeviceIdType.MESH
F32 = jnp.float32
BF16 = jnp.bfloat16
BLOCK = 64
PANEL = 8


def dot(a, b, ca, cb, precision=None):
    return lax.dot_general(
        a, b, (((ca,), (cb,)), ((), ())), precision=precision, preferred_element_type=F32
    )


def split(a):
    high = a.astype(BF16)
    return high, (a - high.astype(F32)).astype(BF16)


def dot3(a, b):
    a0, a1 = split(a)
    b0, b1 = split(b)
    return dot(a0, b0, 1, 0) + (dot(a0, b1, 1, 0) + dot(a1, b0, 1, 0))


def flip(a, mask):
    bit, result = 1, a
    while bit <= mask:
        if mask & bit:
            result = result + bit - 2 * bit * lax.rem(a // bit, 2)
        bit *= 2
    return result


def split_halves(x, low):
    zero = jnp.zeros_like(x)
    return jnp.concatenate([jnp.where(low, x, zero), jnp.where(low, zero, x)], axis=0)


def invert_block(x):
    base = jnp.where(lax.broadcasted_iota(jnp.int32, (PANEL, x.shape[1]), 1) < BLOCK, 0, BLOCK)
    for at in range(0, BLOCK, PANEL):
        picks = [base + (at + i) for i in range(PANEL)]
        rows = x[at : at + PANEL, :]
        cols = [jnp.take_along_axis(rows, pick, axis=1) for pick in picks]
        for i in range(0, PANEL, 2):
            c0, c1 = cols[i], cols[i + 1]
            p00 = 1.0 + c0[i : i + 1, :]
            p01 = c1[i : i + 1, :]
            p11 = 1.0 + c1[i + 1 : i + 2, :]
            inv = 1.0 / (p00 * p11 - p01 * p01)
            m00, m01, m11 = p11 * inv, -p01 * inv, p00 * inv

            def clear(v):
                v0, v1 = v[i : i + 1, :], v[i + 1 : i + 2, :]
                return v - (c0 * (m00 * v0 + m01 * v1) + c1 * (m01 * v0 + m11 * v1))

            rows = clear(rows)
            for j in range(i + 2, PANEL):
                cols[j] = clear(cols[j])
        pieces = []
        for top in range(0, BLOCK, PANEL):
            piece = x[top : top + PANEL, :]
            delta = None
            for i in range(PANEL):
                term = jnp.take_along_axis(piece, picks[i], axis=1) * rows[i : i + 1, :]
                delta = term if delta is None else delta + term
            pieces.append(piece - delta)
        x = jnp.concatenate(pieces, axis=0)
    return x


def kernel(
    nr, nc, resp, tm, sl, ranks, out,
    a_v, om, fr, s_v, s_b, s_t, w_v, b_v, keep, part1, land1, part2, land2,
    a_sem, o_sem, f_sem, s1, r1, s2, r2, s3, r3, s4, r4, s5, r5,
):
    r, c = lax.axis_index("trow"), lax.axis_index("tcol")
    width = a_v.shape[0]
    sketch = tm.shape[1]
    blocks = sketch // BLOCK
    tile_cols = a_v.shape[1] // width
    local = sl.shape[0]
    deep = width // nr
    load_a = pltpu.make_async_copy(resp, a_v, a_sem)
    load_a.start()
    own_om = pltpu.make_async_copy(tm, om.at[r, c], o_sem)
    own_om.start()
    own_fr = pltpu.make_async_copy(sl, fr.at[r], f_sem)
    own_fr.start()
    barrier = pltpu.get_barrier_semaphore()
    for d in range(1, nc):
        pl.semaphore_signal(barrier, inc=1, device_id=(r, lax.rem(c + d, nc)), device_id_type=MESH)
    for e in range(1, nr):
        pl.semaphore_signal(barrier, inc=1, device_id=(lax.rem(r + e, nr), c), device_id_type=MESH)
    pl.semaphore_wait(barrier, nc - 1 + nr - 1)
    first = []
    for d in range(1, nc):
        cp = pltpu.make_async_remote_copy(
            tm, om.at[r, c], s1.at[d - 1], r1.at[d - 1],
            device_id=(r, lax.rem(c + d, nc)), device_id_type=MESH,
        )
        cp.start()
        first.append(cp)
    own_om.wait()
    for cp in first:
        cp.wait_recv()

    mate = r + 1 - 2 * lax.rem(r, 2)
    far = nr // 2

    def shift(e):
        return lax.rem(r + 2 * e, nr)

    def unshift(e):
        return lax.rem(r - 2 * e + nr, nr)

    def push(src, dst, send, recv, n, to):
        cp = pltpu.make_async_remote_copy(
            src, dst, send.at[n], recv.at[n], device_id=(to, c), device_id_type=MESH
        )
        cp.start()
        return cp

    second = [push(om.at[r], om.at[r], s2, r2, e, shift(e)) for e in range(1, far)]
    second.insert(0, push(om.at[r], om.at[r], s2, r2, 0, mate))
    third = [push(sl, fr.at[r], s3, r3, e, shift(e)) for e in range(1, far)]
    third.insert(0, push(sl, fr.at[r], s3, r3, 0, mate))
    load_a.wait()

    def add_block(q, fresh):
        omega = om[q].astype(F32).reshape(deep, sketch).astype(BF16)
        for t in range(tile_cols):
            at = pl.ds(pl.multiple_of(t * width + q * deep, 128), deep)
            term = dot(a_v[:, at], omega, 1, 0)
            s_v[t] = term if fresh else s_v[t] + term

    add_block(r, True)
    for e in range(1, far):
        second[e].wait_recv()
        q = unshift(e)
        second.append(push(om.at[q], om.at[q], s2, r2, far - 1 + e, mate))
    second[0].wait_recv()
    add_block(mate, False)
    for e in range(1, far):
        add_block(unshift(e), False)
    for e in range(1, far):
        second[far - 1 + e].wait_recv()
        q = unshift(e)
        add_block(q + 1 - 2 * lax.rem(q, 2), False)

    slot = lax.broadcasted_iota(jnp.int32, (1, sketch), 1)
    grams = []
    for t in range(tile_cols):
        s = s_v[t]
        norm = jnp.sum(s * s, axis=0, keepdims=True)
        scale = jnp.where(slot < ranks[0, t], lax.rsqrt(norm), 0.0)
        hat = (s * scale).astype(BF16)
        s_b[t] = hat
        turned = hat.T
        s_t[t] = turned
        grams.append(dot(turned, hat, 1, 0))

    half = lax.broadcasted_iota(jnp.int32, (sketch, 2 * BLOCK), 1)
    rows = lax.broadcasted_iota(jnp.int32, (sketch, 2 * BLOCK), 0)
    low = half < BLOCK
    for j in range(blocks):
        x = jnp.concatenate([g[:, j * BLOCK : (j + 1) * BLOCK] for g in grams], axis=1)
        index = jnp.where(low, half, half - BLOCK) + j * BLOCK
        limit = jnp.where(low, ranks[0, 0], ranks[0, 1])
        b_v[j] = jnp.where((rows == index) & (index < limit), x - 1.0, x)

    frames = nr * local

    def apply_frames():
        own_fr.wait()
        third[0].wait_recv()
        for e in range(1, far):
            third[far - 1 + e].wait_recv()
        for t in range(tile_cols):
            s = fr[:, :, t * width : (t + 1) * width].reshape(frames, width)
            y = dot(a_v[:, t * width : (t + 1) * width], s, 1, 1).astype(BF16)
            w_v[t] = dot(s_t[t], y, 1, 0)

    low_b = lax.broadcasted_iota(jnp.int32, (BLOCK, 2 * BLOCK), 1) < BLOCK
    for k in range(blocks):
        span = slice(k * BLOCK, (k + 1) * BLOCK)
        if k == blocks - 1:
            apply_frames()
        square = invert_block(b_v[k, span, :])
        whole_k = b_v[k]
        mid = whole_k - dot3(whole_k, split_halves(square, low_b))
        rights = [split_halves(b_v[j, span, :], low_b) for j in range(blocks)]
        for j in range(blocks):
            b_v[j] = b_v[j] - dot3(mid, rights[j])
        if k == 0:
            for e in range(1, far):
                third[e].wait_recv()
                q = unshift(e)
                third.append(push(fr.at[q], fr.at[q], s3, r3, far - 1 + e, mate))

    full = jnp.concatenate([b_v[j] for j in range(blocks)], axis=1)
    stack = []
    for j in range(blocks):
        span = slice(j * BLOCK, (j + 1) * BLOCK)
        w0, w1 = w_v[0, span, :], w_v[1, span, :]
        zero = jnp.zeros_like(w0)
        stack.append(jnp.concatenate([w0, zero], axis=1))
        stack.append(jnp.concatenate([zero, w1], axis=1))
    corr = dot3(full, jnp.concatenate(stack, axis=0))
    ds = [
        (w_v[t] - corr[:, t * frames : (t + 1) * frames]).astype(BF16) for t in range(tile_cols)
    ]

    share = width // nc
    pairs = nc // 2
    side = lax.rem(c, 2)
    near = c + 1 - 2 * side
    halves = frames // 2
    cuts = [slice(0, halves), slice(halves, frames)]

    def group(n):
        return 2 * flip(c // 2, pairs - 1 - n)

    def chunk(at):
        rows_at = pl.ds(pl.multiple_of(at * share, share), share)
        return sum(dot(s_b[t, rows_at, :], ds[t], 1, 0) for t in range(tile_cols))

    across = []
    for n in range(pairs):
        piece = chunk(group(n) + 1 - side).astype(BF16)
        for h in range(2):
            part1[n, h] = piece[:, cuts[h]]
        keep[n] = chunk(group(n) + side)
        for h in range(2):
            cp = pltpu.make_async_remote_copy(
                part1.at[n, h], land1.at[n, h], s4.at[n, h], r4.at[n, h],
                device_id=(r, near), device_id_type=MESH,
            )
            cp.start()
            across.append(cp)
    along = []
    for n in range(pairs - 1):
        for h in range(2):
            across[2 * n + h].wait_recv()
            part2[n, h] = (keep[n, :, cuts[h]] + land1[n, h].astype(F32)).astype(BF16)
            cp = pltpu.make_async_remote_copy(
                part2.at[n, h], land2.at[n, h], s5.at[n, h], r5.at[n, h],
                device_id=(r, group(n) + side), device_id_type=MESH,
            )
            cp.start()
            along.append(cp)
    for h in range(2):
        across[2 * (pairs - 1) + h].wait_recv()
        total = keep[pairs - 1, :, cuts[h]] + land1[pairs - 1, h].astype(F32)
        for n in range(pairs - 1):
            along[2 * n + h].wait_recv()
            total = total + land2[n, h].astype(F32)
        out[:, cuts[h]] = total
    for cp in first + second + third + across + along:
        cp.wait_send()


def on_device(nr, nc, response, test_matrix, slopes, ranks):
    rows, cols = response.shape
    tile_rows, tile_cols = ranks.shape
    width = rows // tile_rows
    m, sketch = test_matrix.shape
    slopes = slopes.T
    local = slopes.shape[0]
    frames = local * nr
    share = width // nc
    pairs = nc // 2
    dma = pltpu.SemaphoreType.DMA
    return pl.pallas_call(
        functools.partial(kernel, nr, nc),
        out_shape=jax.ShapeDtypeStruct((share, frames), F32),
        in_specs=[
            pl.BlockSpec(memory_space=pl.ANY),
            pl.BlockSpec(memory_space=pltpu.VMEM),
            pl.BlockSpec(memory_space=pltpu.VMEM),
            pl.BlockSpec(memory_space=pltpu.SMEM),
        ],
        out_specs=pl.BlockSpec(memory_space=pltpu.VMEM),
        scratch_shapes=[
            pltpu.VMEM((rows, cols), BF16),
            pltpu.VMEM((nr, nc, m, sketch), BF16),
            pltpu.VMEM((nr, local, cols), BF16),
            pltpu.VMEM((tile_cols, width, sketch), F32),
            pltpu.VMEM((tile_cols, width, sketch), BF16),
            pltpu.VMEM((tile_cols, sketch, width), BF16),
            pltpu.VMEM((tile_cols, sketch, frames), F32),
            pltpu.VMEM((sketch // BLOCK, sketch, 2 * BLOCK), F32),
            pltpu.VMEM((pairs, share, frames), F32),
            pltpu.VMEM((pairs, 2, share, frames // 2), BF16),
            pltpu.VMEM((pairs, 2, share, frames // 2), BF16),
            pltpu.VMEM((pairs - 1, 2, share, frames // 2), BF16),
            pltpu.VMEM((pairs - 1, 2, share, frames // 2), BF16),
            dma, dma, dma,
            dma((nc - 1,)), dma((nc - 1,)),
            dma((nr - 1,)), dma((nr - 1,)),
            dma((nr - 1,)), dma((nr - 1,)),
            dma((pairs, 2)), dma((pairs, 2)),
            dma((pairs - 1, 2)), dma((pairs - 1, 2)),
        ],
        compiler_params=pltpu.CompilerParams(
            collective_id=0, has_side_effects=True, vmem_limit_bytes=60 * 1024 * 1024
        ),
    )(response, test_matrix, slopes, ranks)


def solution(mesh):
    nr, nc = mesh.shape["trow"], mesh.shape["tcol"]
    return jax.shard_map(
        functools.partial(on_device, nr, nc),
        mesh=mesh,
        in_specs=(
            P("trow", "tcol"),
            P(("trow", "tcol"), None),
            P("tcol", "trow"),
            P("trow", "tcol"),
        ),
        out_specs=P(("trow", "tcol"), None),
        check_vma=False,
    )
```

```python
import functools

import jax
import jax.numpy as jnp
from jax import lax
from jax.experimental import pallas as pl
from jax.experimental.pallas import tpu as pltpu
from jax.sharding import PartitionSpec as P

MESH = pl.DeviceIdType.MESH
F32 = jnp.float32
BF16 = jnp.bfloat16
BLOCK = 64
PANEL = 16


def dot(a, b, ca, cb, precision=None):
    return lax.dot_general(
        a, b, (((ca,), (cb,)), ((), ())), precision=precision, preferred_element_type=F32
    )


def split(a):
    high = a.astype(BF16)
    return high, (a - high.astype(F32)).astype(BF16)


def dot3(a, b):
    a0, a1 = split(a)
    b0, b1 = split(b)
    return dot(a0, b0, 1, 0) + (dot(a0, b1, 1, 0) + dot(a1, b0, 1, 0))


def flip(a, mask):
    bit, result = 1, a
    while bit <= mask:
        if mask & bit:
            result = result + bit - 2 * bit * lax.rem(a // bit, 2)
        bit *= 2
    return result


def split_halves(x, low):
    zero = jnp.zeros_like(x)
    return jnp.concatenate([jnp.where(low, x, zero), jnp.where(low, zero, x)], axis=0)


def invert_block(x):
    base = jnp.where(lax.broadcasted_iota(jnp.int32, (PANEL, x.shape[1]), 1) < BLOCK, 0, BLOCK)
    for at in range(0, BLOCK, PANEL):
        picks = [base + (at + i) for i in range(PANEL)]
        rows = x[at : at + PANEL, :]
        cols = [jnp.take_along_axis(rows, pick, axis=1) for pick in picks]
        for i in range(0, PANEL, 2):
            c0, c1 = cols[i], cols[i + 1]
            p00 = 1.0 + c0[i : i + 1, :]
            p01 = c1[i : i + 1, :]
            p11 = 1.0 + c1[i + 1 : i + 2, :]
            inv = 1.0 / (p00 * p11 - p01 * p01)
            m00, m01, m11 = p11 * inv, -p01 * inv, p00 * inv

            def clear(v):
                v0, v1 = v[i : i + 1, :], v[i + 1 : i + 2, :]
                return v - (c0 * (m00 * v0 + m01 * v1) + c1 * (m01 * v0 + m11 * v1))

            rows = clear(rows)
            for j in range(i + 2, PANEL):
                cols[j] = clear(cols[j])
        pieces = []
        for top in range(0, BLOCK, PANEL):
            piece = x[top : top + PANEL, :]
            delta = None
            for i in range(PANEL):
                term = jnp.take_along_axis(piece, picks[i], axis=1) * rows[i : i + 1, :]
                delta = term if delta is None else delta + term
            pieces.append(piece - delta)
        x = jnp.concatenate(pieces, axis=0)
    return x


def kernel(
    nr, nc, resp, tm, sl, ranks, out,
    a_v, om, fr, s_v, s_b, s_t, w_v, b_v, keep, part1, land1, part2, land2,
    a_sem, o_sem, f_sem, s1, r1, s2, r2, s3, r3, s4, r4, s5, r5,
):
    r, c = lax.axis_index("trow"), lax.axis_index("tcol")
    width = a_v.shape[0]
    sketch = tm.shape[1]
    blocks = sketch // BLOCK
    tile_cols = a_v.shape[1] // width
    local = sl.shape[0]
    deep = width // nr
    load_a = pltpu.make_async_copy(resp, a_v, a_sem)
    load_a.start()
    own_om = pltpu.make_async_copy(tm, om.at[r, c], o_sem)
    own_om.start()
    own_fr = pltpu.make_async_copy(sl, fr.at[r], f_sem)
    own_fr.start()
    barrier = pltpu.get_barrier_semaphore()
    for d in range(1, nc):
        pl.semaphore_signal(barrier, inc=1, device_id=(r, lax.rem(c + d, nc)), device_id_type=MESH)
    for e in range(1, nr):
        pl.semaphore_signal(barrier, inc=1, device_id=(lax.rem(r + e, nr), c), device_id_type=MESH)
    pl.semaphore_wait(barrier, nc - 1 + nr - 1)
    first = []
    for d in range(1, nc):
        cp = pltpu.make_async_remote_copy(
            tm, om.at[r, c], s1.at[d - 1], r1.at[d - 1],
            device_id=(r, lax.rem(c + d, nc)), device_id_type=MESH,
        )
        cp.start()
        first.append(cp)
    own_om.wait()
    for cp in first:
        cp.wait_recv()

    mate = r + 1 - 2 * lax.rem(r, 2)
    far = nr // 2

    def shift(e):
        return lax.rem(r + 2 * e, nr)

    def unshift(e):
        return lax.rem(r - 2 * e + nr, nr)

    def push(src, dst, send, recv, n, to):
        cp = pltpu.make_async_remote_copy(
            src, dst, send.at[n], recv.at[n], device_id=(to, c), device_id_type=MESH
        )
        cp.start()
        return cp

    second = [push(om.at[r], om.at[r], s2, r2, e, shift(e)) for e in range(1, far)]
    second.insert(0, push(om.at[r], om.at[r], s2, r2, 0, mate))
    third = [push(sl, fr.at[r], s3, r3, e, shift(e)) for e in range(1, far)]
    third.insert(0, push(sl, fr.at[r], s3, r3, 0, mate))
    load_a.wait()

    def add_block(q, fresh):
        omega = om[q].astype(F32).reshape(deep, sketch).astype(BF16)
        for t in range(tile_cols):
            at = pl.ds(pl.multiple_of(t * width + q * deep, 128), deep)
            term = dot(a_v[:, at], omega, 1, 0)
            s_v[t] = term if fresh else s_v[t] + term

    add_block(r, True)
    for e in range(1, far):
        second[e].wait_recv()
        q = unshift(e)
        second.append(push(om.at[q], om.at[q], s2, r2, far - 1 + e, mate))
    second[0].wait_recv()
    add_block(mate, False)
    for e in range(1, far):
        add_block(unshift(e), False)
    for e in range(1, far):
        second[far - 1 + e].wait_recv()
        q = unshift(e)
        add_block(q + 1 - 2 * lax.rem(q, 2), False)

    slot = lax.broadcasted_iota(jnp.int32, (1, sketch), 1)
    grams = []
    for t in range(tile_cols):
        s = s_v[t]
        norm = jnp.sum(s * s, axis=0, keepdims=True)
        scale = jnp.where(slot < ranks[0, t], lax.rsqrt(norm), 0.0)
        hat = (s * scale).astype(BF16)
        s_b[t] = hat
        turned = hat.T
        s_t[t] = turned
        grams.append(dot(turned, hat, 1, 0))

    half = lax.broadcasted_iota(jnp.int32, (sketch, 2 * BLOCK), 1)
    rows = lax.broadcasted_iota(jnp.int32, (sketch, 2 * BLOCK), 0)
    low = half < BLOCK
    for j in range(blocks):
        x = jnp.concatenate([g[:, j * BLOCK : (j + 1) * BLOCK] for g in grams], axis=1)
        index = jnp.where(low, half, half - BLOCK) + j * BLOCK
        limit = jnp.where(low, ranks[0, 0], ranks[0, 1])
        b_v[j] = jnp.where((rows == index) & (index < limit), x - 1.0, x)

    frames = nr * local

    def apply_frames():
        own_fr.wait()
        third[0].wait_recv()
        for e in range(1, far):
            third[far - 1 + e].wait_recv()
        for t in range(tile_cols):
            s = fr[:, :, t * width : (t + 1) * width].reshape(frames, width)
            y = dot(a_v[:, t * width : (t + 1) * width], s, 1, 1).astype(BF16)
            w_v[t] = dot(s_t[t], y, 1, 0)

    low_b = lax.broadcasted_iota(jnp.int32, (BLOCK, 2 * BLOCK), 1) < BLOCK
    for k in range(blocks):
        span = slice(k * BLOCK, (k + 1) * BLOCK)
        if k == blocks - 1:
            apply_frames()
        square = invert_block(b_v[k, span, :])
        whole_k = b_v[k]
        mid = whole_k - dot3(whole_k, split_halves(square, low_b))
        rights = [split_halves(b_v[j, span, :], low_b) for j in range(blocks)]
        for j in range(blocks):
            b_v[j] = b_v[j] - dot3(mid, rights[j])
        if k == 0:
            for e in range(1, far):
                third[e].wait_recv()
                q = unshift(e)
                third.append(push(fr.at[q], fr.at[q], s3, r3, far - 1 + e, mate))

    ds = []
    for t in range(tile_cols):
        mine = slice(t * BLOCK, (t + 1) * BLOCK)
        full = jnp.concatenate([b_v[j, :, mine] for j in range(blocks)], axis=1)
        w = w_v[t]
        ds.append((w - dot3(full, w)).astype(BF16))

    share = width // nc
    pairs = nc // 2
    side = lax.rem(c, 2)
    near = c + 1 - 2 * side
    halves = frames // 2
    cuts = [slice(0, halves), slice(halves, frames)]

    def group(n):
        return 2 * flip(c // 2, pairs - 1 - n)

    def chunk(at):
        rows_at = pl.ds(pl.multiple_of(at * share, share), share)
        return sum(dot(s_b[t, rows_at, :], ds[t], 1, 0) for t in range(tile_cols))

    across = []
    for n in range(pairs):
        piece = chunk(group(n) + 1 - side).astype(BF16)
        for h in range(2):
            part1[n, h] = piece[:, cuts[h]]
        keep[n] = chunk(group(n) + side)
        for h in range(2):
            cp = pltpu.make_async_remote_copy(
                part1.at[n, h], land1.at[n, h], s4.at[n, h], r4.at[n, h],
                device_id=(r, near), device_id_type=MESH,
            )
            cp.start()
            across.append(cp)
    along = []
    for n in range(pairs - 1):
        for h in range(2):
            across[2 * n + h].wait_recv()
            part2[n, h] = (keep[n, :, cuts[h]] + land1[n, h].astype(F32)).astype(BF16)
            cp = pltpu.make_async_remote_copy(
                part2.at[n, h], land2.at[n, h], s5.at[n, h], r5.at[n, h],
                device_id=(r, group(n) + side), device_id_type=MESH,
            )
            cp.start()
            along.append(cp)
    for h in range(2):
        across[2 * (pairs - 1) + h].wait_recv()
        total = keep[pairs - 1, :, cuts[h]] + land1[pairs - 1, h].astype(F32)
        for n in range(pairs - 1):
            along[2 * n + h].wait_recv()
            total = total + land2[n, h].astype(F32)
        out[:, cuts[h]] = total
    for cp in first + second + third + across + along:
        cp.wait_send()


def on_device(nr, nc, response, test_matrix, slopes, ranks):
    rows, cols = response.shape
    tile_rows, tile_cols = ranks.shape
    width = rows // tile_rows
    m, sketch = test_matrix.shape
    slopes = slopes.T
    local = slopes.shape[0]
    frames = local * nr
    share = width // nc
    pairs = nc // 2
    dma = pltpu.SemaphoreType.DMA
    return pl.pallas_call(
        functools.partial(kernel, nr, nc),
        out_shape=jax.ShapeDtypeStruct((share, frames), F32),
        in_specs=[
            pl.BlockSpec(memory_space=pl.ANY),
            pl.BlockSpec(memory_space=pltpu.VMEM),
            pl.BlockSpec(memory_space=pltpu.VMEM),
            pl.BlockSpec(memory_space=pltpu.SMEM),
        ],
        out_specs=pl.BlockSpec(memory_space=pltpu.VMEM),
        scratch_shapes=[
            pltpu.VMEM((rows, cols), BF16),
            pltpu.VMEM((nr, nc, m, sketch), BF16),
            pltpu.VMEM((nr, local, cols), BF16),
            pltpu.VMEM((tile_cols, width, sketch), F32),
            pltpu.VMEM((tile_cols, width, sketch), BF16),
            pltpu.VMEM((tile_cols, sketch, width), BF16),
            pltpu.VMEM((tile_cols, sketch, frames), F32),
            pltpu.VMEM((sketch // BLOCK, sketch, 2 * BLOCK), F32),
            pltpu.VMEM((pairs, share, frames), F32),
            pltpu.VMEM((pairs, 2, share, frames // 2), BF16),
            pltpu.VMEM((pairs, 2, share, frames // 2), BF16),
            pltpu.VMEM((pairs - 1, 2, share, frames // 2), BF16),
            pltpu.VMEM((pairs - 1, 2, share, frames // 2), BF16),
            dma, dma, dma,
            dma((nc - 1,)), dma((nc - 1,)),
            dma((nr - 1,)), dma((nr - 1,)),
            dma((nr - 1,)), dma((nr - 1,)),
            dma((pairs, 2)), dma((pairs, 2)),
            dma((pairs - 1, 2)), dma((pairs - 1, 2)),
        ],
        compiler_params=pltpu.CompilerParams(
            collective_id=0, has_side_effects=True, vmem_limit_bytes=60 * 1024 * 1024
        ),
    )(response, test_matrix, slopes, ranks)


def solution(mesh):
    nr, nc = mesh.shape["trow"], mesh.shape["tcol"]
    return jax.shard_map(
        functools.partial(on_device, nr, nc),
        mesh=mesh,
        in_specs=(
            P("trow", "tcol"),
            P(("trow", "tcol"), None),
            P("tcol", "trow"),
            P("trow", "tcol"),
        ),
        out_specs=P(("trow", "tcol"), None),
        check_vma=False,
    )
```
